32 devices in a mesh: rows: 4 (over z), chan: 8 (over y, x, core).
Axes of the slice: x: 2, y: 2, z: 4, core: 2. Of those that a mesh axis runs over, the one named last changes fastest.
Arguments:
- feats: bfloat16 [64, 1024, 1024], P('rows', 'chan'), may hold values from -140 to 140
- norm_gain: float32 [1024], P('chan'), may hold values from 0.1 to 1.9
- proj_weight: float32 [8, 1024], P(None, 'chan'), may hold values from -320 to 320
- chan_bias: float32 [1024], P('chan'), may hold values from -8 to -2
Outputs:
- mixed: bfloat16 [64, 1024, 1024], P('rows', 'chan')
The draws below stay inside these ranges and needn't reach their ends.
All inputs are finite; a program needn't handle non-finite values.
Results may differ from the reference program's by a relative error of at most 0.001.
Values sent between devices are 32-bit elements; how exact they have to be, the bound alone decides.
A program may use at most 128 MiB of HBM per device.

```python
import jax
import jax.numpy as jnp
from jax import lax

CHANNELS = 1024
COLS = 1024
HEIGHT = 64


def draw_feats(key, part):
    key_jitter = jax.random.fold_in(key, 11)
    key_base = jax.random.fold_in(key, 12)
    full_shape = (HEIGHT, CHANNELS, COLS)
    channel_index = jnp.arange(CHANNELS, dtype=jnp.float32)
    rising = 10.0 ** (channel_index / max(CHANNELS - 1, 1))
    jitter = jax.random.uniform(key_jitter, (CHANNELS,), jnp.float32, 0.8, 1.25)
    channel_scale = (rising * jitter)[None, :, None]
    values = jnp.clip(jax.random.normal(key_base, full_shape, jnp.float32), -6.0, 6.0) * channel_scale
    return values.astype(jnp.bfloat16)


def draw_proj_weight(key, part):
    key_affinity = jax.random.fold_in(key, 21)
    key_gates = jax.random.fold_in(key, 22)
    affinity_normal = jnp.clip(jax.random.normal(key_affinity, (6, CHANNELS), jnp.float32), -4.0, 4.0)
    affinity = affinity_normal * 1.5
    gates = jnp.clip(jax.random.normal(key_gates, (2, CHANNELS), jnp.float32), -4.0, 4.0)
    return jnp.concatenate([affinity, gates], axis=0)


def level_of(stream_key, dims, shards, least, top_value):
    loudness, own = 1.0, jax.random.fold_in(stream_key, 6)
    for axis_at, blocks in shards:
        draws = jnp.exp(jax.random.uniform(jax.random.fold_in(own, axis_at), (blocks,), jnp.float32, least / len(shards), top_value / len(shards)))
        loudness = loudness * jnp.repeat(draws, dims[axis_at] // blocks).reshape([-1 if axis == axis_at else 1 for axis in range(len(dims))])
    return loudness


def setup_inputs(seed: int = 0) -> dict:
    streams_of = jax.random.split(jax.random.key(seed), 5)
    feats = draw_feats(jax.random.fold_in(streams_of[4], 71), 0)
    norm_gain = jnp.clip(1.0 + 0.18 * jax.random.normal(streams_of[1], (CHANNELS,), jnp.float32), 0.1, 1.9)
    proj_weight = draw_proj_weight(jax.random.fold_in(streams_of[4], 71), 0)
    chan_bias = jnp.clip(-8.0 + 6.0 * jax.random.uniform(streams_of[3], (CHANNELS,), jnp.float32) ** level_of(streams_of[3], (CHANNELS,), ((0, 8),), -0.2, 0.2), -8.0, -2.0)
    return {"feats": feats, "norm_gain": norm_gain, "proj_weight": proj_weight, "chan_bias": chan_bias}


EPSILON = 1e-05

def advance(current, row_weights, row_rate):
    edge_zero = jnp.zeros_like(current[:, :1])
    left_side = jnp.concatenate([edge_zero, current[:, :-1]], axis=1)
    right_side = jnp.concatenate([current[:, 1:], edge_zero], axis=1)
    blended = row_weights[0][None, :] * left_side + row_weights[1][None, :] * current + row_weights[2][None, :] * right_side
    return (1.0 - row_rate) * blended

def normalize(feat_row, norm_gain):
    values = feat_row.astype(jnp.float32)
    square_total = lax.optimization_barrier(jnp.sum(values * values, axis=0))
    inverse = 1.0 / jnp.sqrt(square_total / CHANNELS + EPSILON)
    return values * inverse[None, :] * norm_gain[:, None]

def reference(feats, norm_gain, proj_weight, chan_bias):
    logit_scale = CHANNELS ** (-0.5)

    def row_logits(feat_row):
        normed = normalize(feat_row, norm_gain)
        return jnp.dot(proj_weight, normed, precision=lax.Precision.HIGHEST, preferred_element_type=jnp.float32) * logit_scale
    logits = lax.map(row_logits, feats)

    def make_step(offset):

        def row_step(current, inputs):
            feat_row, logit_row = inputs
            row_weights = jax.nn.softmax(logit_row[offset:offset + 3], axis=0)
            row_rate = jax.nn.sigmoid(logit_row[6 + offset // 3][None, :] + chan_bias[:, None])
            current = advance(current, row_weights, row_rate) + jnp.sqrt(row_rate) * normalize(feat_row, norm_gain)
            return (current, current)
        return row_step
    anchor = jnp.zeros((feats.shape[1], feats.shape[2]), jnp.float32)
    _, down_rows = lax.scan(make_step(0), anchor, (feats, logits))
    upward = make_step(3)

    def up_step(current, inputs):
        feat_row, logit_row, down_row = inputs
        current, _ = upward(current, (feat_row, logit_row))
        return (current, (down_row * current).astype(jnp.bfloat16))
    _, output_rows = lax.scan(up_step, anchor, (feats, logits, down_rows), reverse=True)
    return output_rows
```

```python
import functools

import jax
import jax.numpy as jnp
from jax import lax
from jax.experimental import pallas as pl
from jax.experimental.pallas import tpu as pltpu
from jax.sharding import PartitionSpec as P

EPSILON = 1e-05
LANES = 128
CHUNK = 16
SKEW = 2
UNROLL = 4


def kernel(
    n_rows, n_chan,
    feats, gain_ref, proj_ref, bias_ref,
    out,
    xv, ov, held, in_d, in_u, out_d, out_u,
    part, core_in, half_sum, pieces, final, wst, fac, gain2,
    row_sem, out_sem, s1_send, s1_recv, s2_send, s2_recv, s3_send, s3_recv, s4_send, s4_recv,
    d_send, d_recv, u_send, u_recv,
):
    height, chans, width = xv.shape
    groups = width // LANES
    tiles = height * groups
    half = tiles // 2
    chips = n_chan // 2
    piece = half // chips
    half_rows = height // 2
    total_chans = chans * n_chan
    row_at = lax.axis_index("rows")
    chan_at = lax.axis_index("chan")
    core = lax.rem(chan_at, 2)
    chip = lax.div(chan_at, 2)
    partner = {"chan": chan_at + 1 - 2 * core}

    def same_core(at):
        return {"chan": lax.rem(at, chips) * 2 + core}

    barrier = pltpu.get_barrier_semaphore()
    MESH = pl.DeviceIdType.MESH

    def load_row(r):
        return pltpu.make_async_copy(feats.at[r], xv.at[r], row_sem.at[r])

    def row_order(i):
        return lax.rem(i + (1 - core) * half_rows, height)

    for i in range(height):
        load_row(row_order(i)).start()
    pl.semaphore_signal(barrier, inc=1, device_id=partner, device_id_type=MESH)
    for d in range(1, chips):
        pl.semaphore_signal(barrier, inc=1, device_id=same_core(chip + d), device_id_type=MESH)

    @pl.when(row_at > 0)
    def _():
        pl.semaphore_signal(barrier, inc=1, device_id={"rows": row_at - 1}, device_id_type=MESH)

    @pl.when(row_at < n_rows - 1)
    def _():
        pl.semaphore_signal(barrier, inc=1, device_id={"rows": row_at + 1}, device_id_type=MESH)

    scaled = proj_ref[...] * (gain_ref[...] * (float(total_chans) ** -0.5))
    wst[...] = jnp.zeros_like(wst)
    wst[0:1, :] = scaled[0:1] - scaled[1:2]
    wst[1:2, :] = scaled[2:3] - scaled[1:2]
    wst[2:3, :] = scaled[3:4] - scaled[4:5]
    wst[3:4, :] = scaled[5:6] - scaled[4:5]
    wst[4:6, :] = scaled[6:8]
    whole = wst[0:8, :]
    high = whole.astype(jnp.bfloat16).astype(jnp.float32)
    rest = whole - high
    middle = rest.astype(jnp.bfloat16).astype(jnp.float32)
    wst[0:8, :] = high
    wst[8:16, :] = middle
    wst[16:24, :] = rest - middle
    lhs = wst[...].astype(jnp.bfloat16)
    fac[...] = jnp.exp(-jnp.transpose(jnp.broadcast_to(bias_ref[...], (LANES, chans))))
    gain_all = jnp.transpose(jnp.broadcast_to(gain_ref[...], (LANES, chans)))
    gain2[...] = gain_all * gain_all

    @pl.when(row_at == 0)
    def _():
        in_d[...] = jnp.zeros_like(in_d)

    @pl.when(row_at == n_rows - 1)
    def _():
        in_u[...] = jnp.zeros_like(in_u)

    waits = chips + (row_at > 0).astype(jnp.int32) + (row_at < n_rows - 1).astype(jnp.int32)
    pl.semaphore_wait(barrier, waits)

    quantity = lax.broadcasted_iota(jnp.int32, (8, width), 0)

    def project(i):
        r = row_order(i)
        load_row(r).wait()
        x = xv[r]
        dots = jnp.dot(lhs, x, preferred_element_type=jnp.float32)
        sums = dots[0:8] + (dots[8:16] + dots[16:24])
        xf = x.astype(jnp.float32)
        squares = jnp.sum(xf * xf, axis=0, keepdims=True)
        sums = jnp.where(quantity == 6, jnp.broadcast_to(squares, sums.shape), sums)
        for k in range(groups):
            part[r * groups + k] = sums[:, k * LANES : (k + 1) * LANES]

    per_row = groups

    def project_send(i, _):
        project(i)
        r = row_order(i)
        pltpu.make_async_remote_copy(
            src_ref=part.at[pl.ds(r * per_row, per_row)],
            dst_ref=core_in.at[pl.ds(i * per_row, per_row)],
            send_sem=s1_send, recv_sem=s1_recv, device_id=partner, device_id_type=MESH,
        ).start()
        return 0

    def project_keep(i, _):
        project(i + half_rows)
        return 0

    lax.fori_loop(0, half_rows, project_send, 0)
    lax.fori_loop(0, half_rows, project_keep, 0)

    whole_half = pltpu.make_async_remote_copy(
        src_ref=part.at[pl.ds((1 - core) * half, half)],
        dst_ref=core_in,
        send_sem=s1_send, recv_sem=s1_recv, device_id=partner, device_id_type=MESH,
    )
    whole_half.wait_recv()

    own_half = core * half

    def scatter_copy(d):
        to = lax.rem(chip + d, chips)
        return pltpu.make_async_remote_copy(
            src_ref=half_sum.at[pl.ds(to * piece, piece)],
            dst_ref=pieces.at[d],
            send_sem=s2_send.at[d], recv_sem=s2_recv.at[d],
            device_id=same_core(chip + d), device_id_type=MESH,
        )

    for d in list(range(1, chips)) + [0]:
        to = lax.rem(chip + d, chips) * piece
        half_sum[pl.ds(to, piece)] = part[pl.ds(own_half + to, piece)] + core_in[pl.ds(to, piece)]
        if d:
            scatter_copy(d).start()
    mine = chip * piece
    summed = half_sum[pl.ds(mine, piece)]
    for d in range(1, chips):
        scatter_copy(d).wait_recv()
        summed = summed + pieces[d]
    pieces[0] = summed

    own = own_half + mine

    def logit(q):
        return pieces[0, :, q, :]

    inverse = lax.rsqrt(logit(6) / total_chans + EPSILON)
    for side in range(2):
        before = logit(2 * side) * inverse
        after = logit(2 * side + 1) * inverse
        top = jnp.maximum(jnp.maximum(before, after), 0.0)
        e_before = jnp.exp(before - top)
        e_after = jnp.exp(after - top)
        scale = 1.0 / (e_before + jnp.exp(-top) + e_after)
        final[pl.ds(own, piece), 2 * side, :] = e_before * scale
        final[pl.ds(own, piece), 2 * side + 1, :] = e_after * scale
        final[pl.ds(own, piece), 4 + side, :] = jnp.exp(-(logit(4 + side) * inverse))
    final[pl.ds(own, piece), 6, :] = inverse
    final[pl.ds(own, piece), 7, :] = inverse

    def gather_copy(d):
        return pltpu.make_async_remote_copy(
            src_ref=final.at[pl.ds(own, piece)],
            dst_ref=final.at[pl.ds(own, piece)],
            send_sem=s3_send.at[d], recv_sem=s3_recv.at[d],
            device_id=same_core(chip + d), device_id_type=MESH,
        )

    def forward_copy(d):
        at = own_half + lax.rem(chip + chips - d, chips) * piece
        return pltpu.make_async_remote_copy(
            src_ref=final.at[pl.ds(at, piece)],
            dst_ref=final.at[pl.ds(at, piece)],
            send_sem=s4_send.at[d], recv_sem=s4_recv.at[d],
            device_id=partner, device_id_type=MESH,
        )

    for d in range(1, chips):
        gather_copy(d).start()
    forward_copy(0).start()
    for d in range(1, chips):
        gather_copy(d).wait_recv()
        forward_copy(d).start()
    for d in range(chips):
        forward_copy(d).wait_recv()

    n_chunks = chans // CHUNK
    lane = lax.broadcasted_iota(jnp.int32, (CHUNK, LANES), 1)
    first_lane = lane == 0
    last_lane = lane == LANES - 1

    def sweep(g, side, second, start_ref, end_ref):
        c0 = pl.multiple_of(g * CHUNK, CHUNK)
        channels = pl.ds(c0, CHUNK)
        factor = fac[channels, :]
        gains = gain2[channels, :]

        def step(i, state):
            r = i if side == 0 else height - 1 - i
            rolled_up = [pltpu.roll(v, 1, 1) for v in state]
            rolled_down = [pltpu.roll(v, LANES - 1, 1) for v in state]
            result = []
            for k in range(groups):
                t = r * groups + k
                cols = pl.ds(k * LANES, LANES)
                a0 = final[t, 2 * side : 2 * side + 1, :]
                a2 = final[t, 2 * side + 1 : 2 * side + 2, :]
                a1 = (1.0 - a0) - a2
                e = final[t, 4 + side : 5 + side, :]
                inv = final[t, 6:7, :]
                left_edge = rolled_up[k - 1] if k else jnp.zeros_like(state[k])
                right_edge = rolled_down[k + 1] if k < groups - 1 else jnp.zeros_like(state[k])
                left = jnp.where(first_lane, left_edge, rolled_up[k])
                right = jnp.where(last_lane, right_edge, rolled_down[k])
                root = lax.rsqrt(1.0 + e * factor)
                drive = root * (xv[r, channels, cols].astype(jnp.float32) * inv)
                v = (1.0 - root * root) * (a0 * left + a1 * state[k] + a2 * right) + drive
                if second:
                    product = held[r, channels, cols] * v * gains
                    ov[r, channels, cols] = product.astype(jnp.bfloat16)
                else:
                    held[r, channels, cols] = v
                result.append(v)
            return tuple(result)

        state = tuple(start_ref[channels, pl.ds(k * LANES, LANES)] for k in range(groups))
        state = lax.fori_loop(0, height, step, state, unroll=UNROLL)
        for k in range(groups):
            end_ref[channels, pl.ds(k * LANES, LANES)] = state[k]

    def pass_copy(g, side):
        channels = pl.ds(pl.multiple_of(g * CHUNK, CHUNK), CHUNK)
        src, dst, send, recv = (
            (out_d, in_d, d_send, d_recv) if side == 0 else (out_u, in_u, u_send, u_recv)
        )
        to = jnp.minimum(row_at + 1, n_rows - 1) if side == 0 else jnp.maximum(row_at - 1, 0)
        return pltpu.make_async_remote_copy(
            src_ref=src.at[channels], dst_ref=dst.at[channels],
            send_sem=send.at[g], recv_sem=recv.at[g],
            device_id={"rows": to}, device_id_type=MESH,
        )

    def store_copy(g):
        channels = pl.ds(pl.multiple_of(g * CHUNK, CHUNK), CHUNK)
        return pltpu.make_async_copy(ov.at[:, channels], out.at[:, channels], out_sem.at[g])

    down_first = row_at < n_rows - 1 - row_at

    def turn(s, _):
        for side in range(2):
            away = row_at if side == 0 else n_rows - 1 - row_at
            g = s - away * SKEW
            start_ref, end_ref = (in_d, out_d) if side == 0 else (in_u, out_u)
            is_first = down_first if side == 0 else jnp.logical_not(down_first)

            @pl.when((g >= 0) & (g < n_chunks))
            def _():
                @pl.when(away > 0)
                def _():
                    pass_copy(g, side).wait_recv()

                @pl.when(is_first)
                def _():
                    sweep(g, side, False, start_ref, end_ref)

                @pl.when(jnp.logical_not(is_first))
                def _():
                    sweep(g, side, True, start_ref, end_ref)

                @pl.when(away < n_rows - 1)
                def _():
                    pass_copy(g, side).start()

                @pl.when(jnp.logical_not(is_first))
                def _():
                    store_copy(g).start()

        return 0

    lax.fori_loop(0, n_chunks + (n_rows - 1) * SKEW, turn, 0)

    whole_half.wait_send()
    for d in range(1, chips):
        scatter_copy(d).wait_send()
        gather_copy(d).wait_send()
    for d in range(chips):
        forward_copy(d).wait_send()
    for g in range(n_chunks):
        store_copy(g).wait()

        @pl.when(row_at < n_rows - 1)
        def _():
            pass_copy(g, 0).wait_send()

        @pl.when(row_at > 0)
        def _():
            pass_copy(g, 1).wait_send()


def shards(n_rows, n_chan, feats, norm_gain, proj_weight, chan_bias):
    height, chans, width = feats.shape
    tiles = height * width // LANES
    half = tiles // 2
    chips = n_chan // 2
    piece = half // chips
    n_chunks = chans // CHUNK
    f32 = jnp.float32
    dma = pltpu.SemaphoreType.DMA
    vmem = pl.BlockSpec(memory_space=pltpu.VMEM)
    return pl.pallas_call(
        functools.partial(kernel, n_rows, n_chan),
        out_shape=jax.ShapeDtypeStruct(feats.shape, jnp.bfloat16),
        in_specs=[pl.BlockSpec(memory_space=pl.ANY), vmem, vmem, vmem],
        out_specs=pl.BlockSpec(memory_space=pl.ANY),
        scratch_shapes=[
            pltpu.VMEM(feats.shape, jnp.bfloat16),
            pltpu.VMEM(feats.shape, jnp.bfloat16),
            pltpu.VMEM(feats.shape, f32),
        ]
        + [pltpu.VMEM((chans, width), f32)] * 4
        + [
            pltpu.VMEM((tiles, 8, LANES), f32),
            pltpu.VMEM((half, 8, LANES), f32),
            pltpu.VMEM((half, 8, LANES), f32),
            pltpu.VMEM((chips, piece, 8, LANES), f32),
            pltpu.VMEM((tiles, 8, LANES), f32),
            pltpu.VMEM((32, chans), f32),
            pltpu.VMEM((chans, LANES), f32),
            pltpu.VMEM((chans, LANES), f32),
            dma((height,)), dma((n_chunks,)),
            dma, dma,
            dma((chips,)), dma((chips,)), dma((chips,)), dma((chips,)), dma((chips,)), dma((chips,)),
            dma((n_chunks,)), dma((n_chunks,)), dma((n_chunks,)), dma((n_chunks,)),
        ],
        compiler_params=pltpu.CompilerParams(
            collective_id=0, has_side_effects=True, vmem_limit_bytes=60 * 1024 * 1024
        ),
        name="propagate",
    )(feats, norm_gain.reshape(1, chans), proj_weight, chan_bias.reshape(1, chans))


def solution(mesh):
    in_specs = (P("rows", "chan", None), P("chan"), P(None, "chan"), P("chan"))
    out_specs = P("rows", "chan", None)
    body = functools.partial(shards, mesh.shape["rows"], mesh.shape["chan"])
    return jax.shard_map(body, mesh=mesh, in_specs=in_specs, out_specs=out_specs, check_vma=False)
```

```python
import functools

import jax
import jax.numpy as jnp
from jax import lax
from jax.experimental import pallas as pl
from jax.experimental.pallas import tpu as pltpu
from jax.sharding import PartitionSpec as P

EPSILON = 1e-05
LANES = 128
CHUNK = 32
SKEW = 2
UNROLL = 4


def kernel(
    n_rows, n_chan,
    feats, gain_ref, proj_ref, bias_ref,
    ov,
    xv, held, in_d, in_u, out_d, out_u,
    part, core_in, half_sum, pieces, final, wst, fac, gain2,
    row_sem, s1_send, s1_recv, s2_send, s2_recv, s3_send, s3_recv, s4_send, s4_recv,
    d_send, d_recv, u_send, u_recv,
):
    height, chans, width = xv.shape
    groups = width // LANES
    tiles = height * groups
    half = tiles // 2
    chips = n_chan // 2
    piece = half // chips
    half_rows = height // 2
    total_chans = chans * n_chan
    row_at = lax.axis_index("rows")
    chan_at = lax.axis_index("chan")
    core = lax.rem(chan_at, 2)
    chip = lax.div(chan_at, 2)
    partner = {"chan": chan_at + 1 - 2 * core}

    def same_core(at):
        return {"chan": lax.rem(at, chips) * 2 + core}

    barrier = pltpu.get_barrier_semaphore()
    MESH = pl.DeviceIdType.MESH

    def load_row(r):
        return pltpu.make_async_copy(feats.at[r], xv.at[r], row_sem.at[r])

    def row_order(i):
        return lax.rem(i + (1 - core) * half_rows, height)

    for i in range(height):
        load_row(row_order(i)).start()
    pl.semaphore_signal(barrier, inc=1, device_id=partner, device_id_type=MESH)
    for d in range(1, chips):
        pl.semaphore_signal(barrier, inc=1, device_id=same_core(chip + d), device_id_type=MESH)

    @pl.when(row_at > 0)
    def _():
        pl.semaphore_signal(barrier, inc=1, device_id={"rows": row_at - 1}, device_id_type=MESH)

    @pl.when(row_at < n_rows - 1)
    def _():
        pl.semaphore_signal(barrier, inc=1, device_id={"rows": row_at + 1}, device_id_type=MESH)

    scaled = proj_ref[...] * (gain_ref[...] * (float(total_chans) ** -0.5))
    wst[...] = jnp.zeros_like(wst)
    wst[0:1, :] = scaled[0:1] - scaled[1:2]
    wst[1:2, :] = scaled[2:3] - scaled[1:2]
    wst[2:3, :] = scaled[3:4] - scaled[4:5]
    wst[3:4, :] = scaled[5:6] - scaled[4:5]
    wst[4:6, :] = scaled[6:8]
    whole = wst[0:8, :]
    high = whole.astype(jnp.bfloat16).astype(jnp.float32)
    rest = whole - high
    middle = rest.astype(jnp.bfloat16).astype(jnp.float32)
    wst[0:8, :] = high
    wst[8:16, :] = middle
    wst[16:24, :] = rest - middle
    lhs = wst[...].astype(jnp.bfloat16)
    fac[...] = jnp.exp(-jnp.transpose(jnp.broadcast_to(bias_ref[...], (LANES, chans))))
    gain_all = jnp.transpose(jnp.broadcast_to(gain_ref[...], (LANES, chans)))
    gain2[...] = gain_all * gain_all

    @pl.when(row_at == 0)
    def _():
        in_d[...] = jnp.zeros_like(in_d)

    @pl.when(row_at == n_rows - 1)
    def _():
        in_u[...] = jnp.zeros_like(in_u)

    waits = chips + (row_at > 0).astype(jnp.int32) + (row_at < n_rows - 1).astype(jnp.int32)
    pl.semaphore_wait(barrier, waits)

    quantity = lax.broadcasted_iota(jnp.int32, (8, width), 0)

    def project(i):
        r = row_order(i)
        load_row(r).wait()
        x = xv[r]
        dots = jnp.dot(lhs, x, preferred_element_type=jnp.float32)
        sums = dots[0:8] + (dots[8:16] + dots[16:24])
        xf = x.astype(jnp.float32)
        squares = jnp.sum(xf * xf, axis=0, keepdims=True)
        sums = jnp.where(quantity == 6, jnp.broadcast_to(squares, sums.shape), sums)
        for k in range(groups):
            part[r * groups + k] = sums[:, k * LANES : (k + 1) * LANES]

    per_row = groups

    def project_send(i, _):
        project(i)
        r = row_order(i)
        pltpu.make_async_remote_copy(
            src_ref=part.at[pl.ds(r * per_row, per_row)],
            dst_ref=core_in.at[pl.ds(i * per_row, per_row)],
            send_sem=s1_send, recv_sem=s1_recv, device_id=partner, device_id_type=MESH,
        ).start()
        return 0

    def project_keep(i, _):
        project(i + half_rows)
        return 0

    lax.fori_loop(0, half_rows, project_send, 0)
    lax.fori_loop(0, half_rows, project_keep, 0)

    whole_half = pltpu.make_async_remote_copy(
        src_ref=part.at[pl.ds((1 - core) * half, half)],
        dst_ref=core_in,
        send_sem=s1_send, recv_sem=s1_recv, device_id=partner, device_id_type=MESH,
    )
    whole_half.wait_recv()

    own_half = core * half

    def scatter_copy(d):
        to = lax.rem(chip + d, chips)
        return pltpu.make_async_remote_copy(
            src_ref=half_sum.at[pl.ds(to * piece, piece)],
            dst_ref=pieces.at[d],
            send_sem=s2_send.at[d], recv_sem=s2_recv.at[d],
            device_id=same_core(chip + d), device_id_type=MESH,
        )

    for d in list(range(1, chips)) + [0]:
        to = lax.rem(chip + d, chips) * piece
        half_sum[pl.ds(to, piece)] = part[pl.ds(own_half + to, piece)] + core_in[pl.ds(to, piece)]
        if d:
            scatter_copy(d).start()
    mine = chip * piece
    summed = half_sum[pl.ds(mine, piece)]
    for d in range(1, chips):
        scatter_copy(d).wait_recv()
        summed = summed + pieces[d]
    pieces[0] = summed

    own = own_half + mine

    def logit(q):
        return pieces[0, :, q, :]

    inverse = lax.rsqrt(logit(6) / total_chans + EPSILON)
    for side in range(2):
        before = logit(2 * side) * inverse
        after = logit(2 * side + 1) * inverse
        top = jnp.maximum(jnp.maximum(before, after), 0.0)
        e_before = jnp.exp(before - top)
        e_after = jnp.exp(after - top)
        scale = 1.0 / (e_before + jnp.exp(-top) + e_after)
        final[pl.ds(own, piece), 2 * side, :] = e_before * scale
        if side == 0:
            final[pl.ds(own, piece), 7, :] = jnp.exp(-top) * scale
        final[pl.ds(own, piece), 2 * side + 1, :] = e_after * scale
        final[pl.ds(own, piece), 4 + side, :] = jnp.exp(-(logit(4 + side) * inverse))
    final[pl.ds(own, piece), 6, :] = inverse

    def gather_copy(d):
        return pltpu.make_async_remote_copy(
            src_ref=final.at[pl.ds(own, piece)],
            dst_ref=final.at[pl.ds(own, piece)],
            send_sem=s3_send.at[d], recv_sem=s3_recv.at[d],
            device_id=same_core(chip + d), device_id_type=MESH,
        )

    def forward_copy(d):
        at = own_half + lax.rem(chip + chips - d, chips) * piece
        return pltpu.make_async_remote_copy(
            src_ref=final.at[pl.ds(at, piece)],
            dst_ref=final.at[pl.ds(at, piece)],
            send_sem=s4_send.at[d], recv_sem=s4_recv.at[d],
            device_id=partner, device_id_type=MESH,
        )

    for d in range(1, chips):
        gather_copy(d).start()
    forward_copy(0).start()
    for d in range(1, chips):
        gather_copy(d).wait_recv()
        forward_copy(d).start()
    for d in range(chips):
        forward_copy(d).wait_recv()

    n_chunks = chans // CHUNK
    lane = lax.broadcasted_iota(jnp.int32, (CHUNK, LANES), 1)
    first_lane = lane == 0
    last_lane = lane == LANES - 1

    def weight(t, q):
        return final[t, pl.ds(q, 8, stride=0), :]

    def sweep(g, side, second, start_ref, end_ref):
        c0 = pl.multiple_of(g * CHUNK, CHUNK)
        channels = pl.ds(c0, CHUNK)
        factor = fac[channels, :]
        gains = gain2[channels, :]

        def step(i, state):
            r = i if side == 0 else height - 1 - i
            rolled_up = [pltpu.roll(v, 1, 1) for v in state]
            rolled_down = [pltpu.roll(v, LANES - 1, 1) for v in state]
            result = []
            for k in range(groups):
                t = r * groups + k
                cols = pl.ds(k * LANES, LANES)
                a0 = weight(t, 2 * side)
                a2 = weight(t, 2 * side + 1)
                a1 = (1.0 - a0) - a2 if side else weight(t, 7)
                a0, a1, a2, e, inv = (
                    jnp.concatenate([one] * (CHUNK // 8), axis=0)
                    for one in (a0, a1, a2, weight(t, 4 + side), weight(t, 6))
                )
                left_edge = rolled_up[k - 1] if k else jnp.zeros_like(state[k])
                right_edge = rolled_down[k + 1] if k < groups - 1 else jnp.zeros_like(state[k])
                left = jnp.where(first_lane, left_edge, rolled_up[k])
                right = jnp.where(last_lane, right_edge, rolled_down[k])
                root = lax.rsqrt(1.0 + e * factor)
                normed = xv[r, channels, cols].astype(jnp.float32) * inv
                blended = a0 * left + a1 * state[k] + a2 * right
                v = blended + root * (normed - root * blended)
                if second:
                    product = held[r, channels, cols] * v * gains
                    ov[r, channels, cols] = product.astype(jnp.bfloat16)
                else:
                    held[r, channels, cols] = v
                result.append(v)
            return tuple(result)

        state = tuple(start_ref[channels, pl.ds(k * LANES, LANES)] for k in range(groups))
        state = lax.fori_loop(0, height, step, state, unroll=UNROLL)
        for k in range(groups):
            end_ref[channels, pl.ds(k * LANES, LANES)] = state[k]

    def pass_copy(g, side):
        channels = pl.ds(pl.multiple_of(g * CHUNK, CHUNK), CHUNK)
        src, dst, send, recv = (
            (out_d, in_d, d_send, d_recv) if side == 0 else (out_u, in_u, u_send, u_recv)
        )
        to = jnp.minimum(row_at + 1, n_rows - 1) if side == 0 else jnp.maximum(row_at - 1, 0)
        return pltpu.make_async_remote_copy(
            src_ref=src.at[channels], dst_ref=dst.at[channels],
            send_sem=send.at[g], recv_sem=recv.at[g],
            device_id={"rows": to}, device_id_type=MESH,
        )

    down_first = row_at < n_rows - 1 - row_at

    def turn(s, _):
        for side in range(2):
            away = row_at if side == 0 else n_rows - 1 - row_at
            g = s - away * SKEW
            start_ref, end_ref = (in_d, out_d) if side == 0 else (in_u, out_u)
            is_first = down_first if side == 0 else jnp.logical_not(down_first)

            @pl.when((g >= 0) & (g < n_chunks))
            def _():
                @pl.when(away > 0)
                def _():
                    pass_copy(g, side).wait_recv()

                @pl.when(is_first)
                def _():
                    sweep(g, side, False, start_ref, end_ref)

                @pl.when(jnp.logical_not(is_first))
                def _():
                    sweep(g, side, True, start_ref, end_ref)

                @pl.when(away < n_rows - 1)
                def _():
                    pass_copy(g, side).start()

        return 0

    lax.fori_loop(0, n_chunks + (n_rows - 1) * SKEW, turn, 0)

    whole_half.wait_send()
    for d in range(1, chips):
        scatter_copy(d).wait_send()
        gather_copy(d).wait_send()
    for d in range(chips):
        forward_copy(d).wait_send()
    for g in range(n_chunks):
        @pl.when(row_at < n_rows - 1)
        def _():
            pass_copy(g, 0).wait_send()

        @pl.when(row_at > 0)
        def _():
            pass_copy(g, 1).wait_send()


def shards(n_rows, n_chan, feats, norm_gain, proj_weight, chan_bias):
    height, chans, width = feats.shape
    tiles = height * width // LANES
    half = tiles // 2
    chips = n_chan // 2
    piece = half // chips
    n_chunks = chans // CHUNK
    f32 = jnp.float32
    dma = pltpu.SemaphoreType.DMA
    vmem = pl.BlockSpec(memory_space=pltpu.VMEM)
    return pl.pallas_call(
        functools.partial(kernel, n_rows, n_chan),
        out_shape=pltpu.VMEM(feats.shape, jnp.bfloat16),
        in_specs=[pl.BlockSpec(memory_space=pl.ANY), vmem, vmem, vmem],
        out_specs=pl.BlockSpec(memory_space=pltpu.VMEM),
        scratch_shapes=[
            pltpu.VMEM(feats.shape, jnp.bfloat16),
            pltpu.VMEM(feats.shape, f32),
        ]
        + [pltpu.VMEM((chans, width), f32)] * 4
        + [
            pltpu.VMEM((tiles, 8, LANES), f32),
            pltpu.VMEM((half, 8, LANES), f32),
            pltpu.VMEM((half, 8, LANES), f32),
            pltpu.VMEM((chips, piece, 8, LANES), f32),
            pltpu.VMEM((tiles, 8, LANES), f32),
            pltpu.VMEM((32, chans), f32),
            pltpu.VMEM((chans, LANES), f32),
            pltpu.VMEM((chans, LANES), f32),
            dma((height,)),
            dma, dma,
            dma((chips,)), dma((chips,)), dma((chips,)), dma((chips,)), dma((chips,)), dma((chips,)),
            dma((n_chunks,)), dma((n_chunks,)), dma((n_chunks,)), dma((n_chunks,)),
        ],
        compiler_params=pltpu.CompilerParams(
            collective_id=0, has_side_effects=True, vmem_limit_bytes=56 * 1024 * 1024
        ),
        name="propagate",
    )(feats, norm_gain.reshape(1, chans), proj_weight, chan_bias.reshape(1, chans))


def solution(mesh):
    in_specs = (P("rows", "chan", None), P("chan"), P(None, "chan"), P("chan"))
    out_specs = P("rows", "chan", None)
    body = functools.partial(shards, mesh.shape["rows"], mesh.shape["chan"])
    return jax.shard_map(body, mesh=mesh, in_specs=in_specs, out_specs=out_specs, check_vma=False)
```
